32 devices in a mesh: group: 2 (over y), swap: 8 (over z, x), image: 2 (over core).
Axes of the slice: x: 2, y: 2, z: 4, core: 2. Of those that a mesh axis runs over, the one named last changes fastest.
Arguments:
- images_in: bfloat16 [16, 1536, 4096], P(('group', 'image'), 'swap'), parts along dimension 0, may hold values from -6 to 6
- kernel: bfloat16 [1536, 49], P('swap'), may hold values from -1.75 to 1.75
- conv_bias: float32 [1536], P('swap'), may hold values from -1 to 1
- norm_gain: float32 [1536], replicated, may hold values from 0.1 to 1.9
- norm_shift: float32 [1536], replicated, may hold values from -0.5 to 0.5
- fp8_weight: bfloat16 [1536, 6144], P('swap', 'image'), may hold values from -1.875 to 1.875, as said below
- block_scale: int32 [1536, 48], P('swap', 'image'), may hold values from -7 to -5
- adapter_a: bfloat16 [1536, 32], replicated, may hold values from -0.15625 to 0.15625
- adapter_b: bfloat16 [32, 6144], P(None, 'image'), may hold values from -0.25 to 0.25
- cotangent: bfloat16 [16, 4096, 6144], P('group', 'swap', 'image'), parts along dimension 0, may hold values from -0.05 to 0.05
Outputs:
- grad_a: float32 [3072, 32], P('group'), parts along dimension 0
- grad_b: float32 [64, 6144], P('group', 'image'), parts along dimension 0
The draws below stay inside these ranges and needn't reach their ends.
There are 2 independent parts, one for each index of `group`. The reference program is written for one: setup_inputs(seed, part) draws one part's arguments, and reference() takes and returns one part's arrays. A program takes and returns all parts, laid end to end along the dimension named above; an argument that names none is the same for every part. Nothing has to cross between parts.
Inputs may be any that keep to these rules, and one draw needn't show every extreme that they name: `fp8_weight`: each entry is a value of the E4M3 format: a sign times 2 to an integer power times 1 + k / 8 for an integer k of 0 to 7. `block_scale`: the entry at [c, j] is the exponent of the scale of hidden units 128 * j to 128 * j + 127 of weight row c.
All inputs are finite; a program needn't handle non-finite values.
Results may differ from the reference program's by a relative error of at most 0.00055.
The reference program's roundings to bfloat16 on the way (of `conv`, `normed`, `scaled_weight`, `low_rank` and `grad_pre`) count: a program that leaves them out, or rounds other values in their place, can miss the bound.
Values may be sent and summed in bfloat16 or wider, within the bound.
A program may use at most 192 MiB of HBM per device.

```python
import math
import jax
import jax.numpy as jnp
from jax import lax

C = 1536
FF = 6144
R = 32
KS = 7
H = 64
W = 64
IMAGES = 8


def draw_kernel(key, part):
    first_key, second_key = jax.random.split(key)
    spread = jnp.exp(jax.random.uniform(second_key, (C, 1), jnp.float32, math.log(0.3), math.log(3.0)))
    values = jnp.clip(jax.random.normal(first_key, (C, KS * KS), jnp.float32), -4.0, 4.0)
    return (values * spread / KS).astype(jnp.bfloat16)


def draw_fp8_weight(key, part):
    sign_key, power_key, mantissa_key = jax.random.split(key, 3)
    lowest = -2
    negative = jax.random.bernoulli(sign_key, 0.5, (C, FF))
    exponent = jax.random.randint(power_key, (C, FF), lowest, 1)
    mantissa = jax.random.randint(mantissa_key, (C, FF), 0, 8)
    power = jnp.where(exponent == -3, 0.125, jnp.where(exponent == -2, 0.25, jnp.where(exponent == -1, 0.5, 1.0)))
    signs = jnp.where(negative, -1.0, 1.0)
    values = signs * power * (1.0 + mantissa.astype(jnp.float32) / 8.0)
    return values.astype(jnp.float32).astype(jnp.bfloat16)


def draw_cotangent(key, part):
    value_key, scale_key = jax.random.split(key, 2)
    shape = (IMAGES, H * W, FF)
    row_scale = jnp.exp(jax.random.uniform(scale_key, (IMAGES, H * W, 1), jnp.float32, 0.0, math.log(10.0)))
    values = jnp.clip(jax.random.normal(value_key, shape, jnp.float32), -4.0, 4.0)
    return (values * row_scale / 1024.0).astype(jnp.bfloat16)


def place_ends(entries, stream_key, least, largest):
    place = [jax.random.randint(jax.random.fold_in(stream_key, axis), (), 0, length) for axis, length in enumerate(entries.shape)]
    main_axis = entries.shape.index(max(entries.shape))
    beside = place[:main_axis] + [(place[main_axis] + 1) % entries.shape[main_axis]] + place[main_axis + 1:]
    return entries.at[tuple(place)].set(least).at[tuple(beside)].set(largest)


def steps_of(stream_key, extent, cuts, least, largest):
    level, own = 1.0, jax.random.fold_in(stream_key, 6)
    for position, shards_of in cuts:
        draws = jnp.exp(jax.random.uniform(jax.random.fold_in(own, position), (shards_of,), jnp.float32, least / len(cuts), largest / len(cuts)))
        level = level * jnp.repeat(draws, extent[position] // shards_of).reshape([-1 if axis == position else 1 for axis in range(len(extent))])
    return level


def noise(rng, dims, width, most, pieces=(), dtype=jnp.bfloat16):
    loudness = steps_of(rng, dims, pieces, -0.22, 0.18) if pieces else 1.0
    result = jax.random.normal(rng, dims, jnp.float32) * width * loudness
    return jnp.minimum(jnp.maximum(result, -most), most).astype(dtype)


def setup_inputs(seed: int = 0, part: int = 0) -> dict:
    key_list = jax.random.split(jax.random.key(seed), 11)
    own_keys = jax.random.split(jax.random.fold_in(key_list[10], part), 11)
    images_in = noise(own_keys[0], (IMAGES, C, H * W), 1.0, 6.0, ((0, 2), (1, 8)))
    kernel = draw_kernel(jax.random.fold_in(key_list[10], 71), part)
    conv_bias = jnp.clip(jax.random.uniform(key_list[2], (C,), jnp.float32, -1.0, 1.0) * steps_of(key_list[2], (C,), ((0, 8),), -0.4, 0.0), -1.0, 1.0)
    norm_gain = jnp.clip(1.0 + 0.18 * jax.random.normal(key_list[3], (C,), jnp.float32), 0.1, 1.9)
    norm_shift = jnp.clip(jax.random.uniform(key_list[4], (C,), jnp.float32, -0.5, 0.5), -0.5, 0.5)
    fp8_weight = draw_fp8_weight(jax.random.fold_in(key_list[10], 71), part)
    block_scale = place_ends(jax.random.randint(key_list[6], (C, FF // 128), -7, -4), jax.random.fold_in(key_list[6], 1), -7, (-4) - 1).astype(jnp.int32)
    adapter_a = noise(key_list[7], (C, R), C ** -0.5, 0.15625)
    adapter_b = noise(key_list[8], (R, FF), (R * 16) ** -0.5, 0.25, ((1, 2),))
    cotangent = draw_cotangent(jax.random.fold_in(jax.random.fold_in(key_list[10], part), 71), part)
    return {"images_in": images_in, "kernel": kernel, "conv_bias": conv_bias, "norm_gain": norm_gain, "norm_shift": norm_shift, "fp8_weight": fp8_weight, "block_scale": block_scale, "adapter_a": adapter_a, "adapter_b": adapter_b, "cotangent": cotangent}


adapter_scale = 2.0
norm_eps = 1e-06

def power_table(scales):
    factor = jnp.zeros(scales.shape, jnp.float32)
    for exponent in range(-12, 4):
        factor = factor + jnp.where(scales == exponent, jnp.float32(2.0 ** exponent), jnp.float32(0.0))
    return factor

def decode(weight, scales):
    row_count = weight.shape[0]
    groups = scales.shape[1]
    blocks = weight.reshape(row_count, groups, -1).astype(jnp.float32) * power_table(scales)[:, :, None]
    return blocks.reshape(row_count, -1).astype(jnp.bfloat16)

def gelu_slope(pre_act):
    cumulative = 0.5 * (1.0 + jax.scipy.special.erf(pre_act * 0.7071067811865476))
    density = jnp.exp(-0.5 * pre_act * pre_act) * 0.3989422804014327
    return cumulative + pre_act * density

def depthwise(images, kernel, conv_bias, map_width):
    pixels = images.shape[-1]
    last_axis = images.ndim - 1
    half_span = KS // 2
    margin = half_span * map_width + half_span
    padded = jnp.pad(images, [(0, 0)] * last_axis + [(margin, margin)])
    column = jnp.arange(pixels) % map_width
    weights = kernel.astype(jnp.float32)
    summed = jnp.zeros(images.shape, jnp.float32)
    for row_step in range(KS):
        for col_step in range(KS):
            offset = (row_step - half_span) * map_width + (col_step - half_span)
            shifted = lax.slice_in_dim(padded, margin + offset, margin + offset + pixels, axis=last_axis)
            moved = column + (col_step - half_span)
            inside = ((moved >= 0) & (moved < map_width)).astype(jnp.float32)
            summed = summed + shifted.astype(jnp.float32) * weights[:, row_step * KS + col_step][:, None] * inside
    return summed + conv_bias.astype(jnp.float32)[:, None]

def reference(images_in, kernel, conv_bias, norm_gain, norm_shift, fp8_weight, block_scale, adapter_a, adapter_b, cotangent):
    scaled_weight = decode(fp8_weight, block_scale)

    def one_image(carry, inputs):
        image, upstream = inputs
        conv = depthwise(image, kernel, conv_bias, W).astype(jnp.bfloat16)
        values = conv.astype(jnp.float32)
        average = lax.optimization_barrier(jnp.mean(values, axis=0, keepdims=True))
        centred = values - average
        variance = lax.optimization_barrier(jnp.mean(centred * centred, axis=0, keepdims=True))
        scaled = centred * lax.rsqrt(variance + norm_eps) * norm_gain[:, None] + norm_shift[:, None]
        normed = scaled.T.astype(jnp.bfloat16)
        low_rank = jnp.dot(normed, adapter_a, preferred_element_type=jnp.float32).astype(jnp.bfloat16)
        pre_act = jnp.dot(normed, scaled_weight, preferred_element_type=jnp.float32)
        pre_act = pre_act + adapter_scale * jnp.dot(low_rank, adapter_b, preferred_element_type=jnp.float32)
        grad_pre = (upstream.astype(jnp.float32) * gelu_slope(pre_act)).astype(jnp.bfloat16)
        grad_b = adapter_scale * jnp.dot(low_rank.T, grad_pre, preferred_element_type=jnp.float32)
        back_low = jnp.dot(grad_pre, adapter_b.T, preferred_element_type=jnp.float32)
        grad_a = adapter_scale * jnp.dot(normed.astype(jnp.float32).T, back_low, precision=lax.Precision.HIGHEST)
        return ((carry[0] + grad_a, carry[1] + grad_b), None)
    initial = (jnp.zeros((C, R), jnp.float32), jnp.zeros((R, FF), jnp.float32))
    totals, unused = lax.scan(one_image, initial, (images_in, cotangent))
    return (totals[0], totals[1])
```

```python
import functools

import jax
import jax.numpy as jnp
import numpy as np
from jax import lax
from jax.experimental import pallas as pl
from jax.experimental.pallas import tpu as pltpu
from jax.sharding import PartitionSpec as P

KS = 7
W = 64
HALF = KS // 2
MESH = pl.DeviceIdType.MESH
CH = 16
LANES = 2 * W
QUARTERS = 4
STEP = 512


adapter_scale = 2.0
norm_eps = 1e-06


def power_table(scales):
    factor = jnp.zeros(scales.shape, jnp.float32)
    for exponent in range(-12, 4):
        factor = factor + jnp.where(
            scales == exponent, jnp.float32(2.0**exponent), jnp.float32(0.0)
        )
    return factor


def decode(weight, scales):
    row_count = weight.shape[0]
    groups = scales.shape[1]
    blocks = (
        weight.reshape(row_count, groups, -1).astype(jnp.float32) * power_table(scales)[:, :, None]
    )
    return blocks.reshape(row_count, -1).astype(jnp.bfloat16)


def gelu_slope(pre_act):
    cumulative = 0.5 * (1.0 + lax.erf(pre_act * 0.7071067811865476))
    density = jnp.exp(-0.5 * pre_act * pre_act) * 0.3989422804014327
    return cumulative + pre_act * density


def band_table():
    table = np.zeros((KS * KS, (KS + 1) * LANES), np.float32)
    for s in range(KS + 1):
        for r in range(2):
            a = s - r
            if 0 <= a < KS:
                for b in range(KS):
                    table[a * KS + b, s * LANES + (r * W + HALF - b) % LANES] = 1.0
    return table


def band_mask():
    rows = np.arange(W)[:, None]
    lanes = np.arange(LANES)[None, :] % W
    return (np.abs(rows - lanes) <= HALF).astype(np.float32)


def flip(me, bits):
    out = me
    d = 1
    while d <= bits:
        if bits & d:
            out = out + d - 2 * d * lax.rem(me // d, 2)
        d *= 2
    return out


def conv_chunk(xb, rows, u, mask_ref, bias_ref, xf, yf, put):
    images, ch, pixels = xb.shape
    pairs = pixels // LANES
    span = pairs + 3
    for i in range(images):
        x = xb[i].astype(jnp.float32)
        x = jnp.concatenate([x, jnp.zeros((ch, LANES), jnp.float32)], axis=1)
        x = pltpu.roll(x, W, axis=1)
        for g in range(pairs + 1):
            xf[pl.ds((i * span + g + 1) * ch, ch), :] = x[:, g * LANES : (g + 1) * LANES]
    mask = mask_ref[...]
    for c in range(ch):
        bands = []
        for s in range(KS + 1):
            first = jnp.broadcast_to(u[s, pl.ds(rows + c, 1), :], (W, LANES))
            band = pltpu.roll(first, 0, 1, stride=1, stride_axis=0) * mask
            bands.append(band.astype(jnp.bfloat16))
        parts = []
        for i in range(images):
            moved = [
                xf[pl.ds((i * span + j) * ch + c, pairs, stride=ch), :].astype(jnp.bfloat16)
                for j in range((KS + 1) // 2)
            ]
            parts.append(jnp.concatenate(moved, axis=1))
        y = jnp.dot(
            jnp.concatenate(parts, axis=0),
            jnp.concatenate(bands, axis=0),
            preferred_element_type=jnp.float32,
        )
        yf[pl.ds(c, images * pairs, stride=ch), :] = y
    bias = jnp.broadcast_to(bias_ref[pl.ds(rows, ch), :], (ch, LANES))
    for i in range(images):
        for g in range(pairs):
            put(i, g, (yf[pl.ds((i * pairs + g) * ch, ch), :] + bias).astype(jnp.bfloat16))


def low_bit(x):
    return x & -x


def lower(x, n):
    hops = []
    d = (low_bit(x) if x else n) // 2
    while d >= 1:
        hops.append(d)
        d //= 2
    return hops


def fused_kernel(
    n,
    x_hbm,
    k_ref,
    bias_ref,
    table_ref,
    mask_ref,
    w_ref,
    cot_hbm,
    a_ref,
    b_ref,
    gain_ref,
    shift_ref,
    oa_ref,
    ob_ref,
    xb,
    u,
    xf,
    yf,
    stage,
    conv,
    weight,
    cot,
    tok,
    grads,
    ga_ref,
    gb_ref,
    pair,
    held,
    parts,
    total,
    x_sem,
    cot_sem,
    own_sem,
    w_own_sem,
    early_send,
    early_recv,
    late_send,
    late_recv,
    w_send,
    w_recv,
    y_send,
    y_recv,
    f_send,
    f_recv,
    pair_sem,
    s1,
    r1,
    s2,
    r2,
):
    images, channels, pixels = x_hbm.shape
    piece = pixels // n
    hidden = w_ref.shape[1]
    depth = channels * n
    chunks = channels // CH
    quarter = channels // QUARTERS
    me = lax.axis_index("swap")
    core = lax.axis_index("image")
    other = 1 - core
    group = lax.axis_index("group")

    def x_load(q):
        slot = lax.rem(q, 2)
        return pltpu.make_async_copy(
            x_hbm.at[:, pl.ds(pl.multiple_of(q * CH, CH), CH), :], xb.at[slot], x_sem.at[slot]
        )

    def cot_load(unit):
        slot = lax.rem(unit, 2)
        image = lax.rem(core + lax.rem(unit, 2), 2) * images + unit // 2
        return pltpu.make_async_copy(cot_hbm.at[image], cot.at[slot], cot_sem.at[slot])

    x_load(0).start()
    x_load(1).start()
    barrier = pltpu.get_barrier_semaphore()
    for k in range(1, n):
        pl.semaphore_signal(
            barrier, inc=1, device_id={"swap": flip(me, k)}, device_id_type=MESH
        )
    pl.semaphore_signal(barrier, inc=1, device_id={"image": other}, device_id_type=MESH)
    pl.semaphore_signal(barrier, inc=1, device_id={"group": 1 - group}, device_id_type=MESH)

    zero = jnp.zeros((CH, LANES), jnp.float32)
    span = pixels // LANES + 3
    for i in range(images):
        xf[pl.ds(i * span * CH, CH), :] = zero
        xf[pl.ds((i * span + span - 1) * CH, CH), :] = zero
    for s in range(KS + 1):
        u[s] = jnp.dot(
            k_ref[...],
            table_ref[:, s * LANES : (s + 1) * LANES],
            preferred_element_type=jnp.float32,
        )
    ga_ref[...] = jnp.zeros_like(ga_ref)
    gb_ref[...] = jnp.zeros_like(gb_ref)
    weight[depth:, :] = b_ref[...]
    pl.semaphore_wait(barrier, n + 1)

    share = channels // 2

    def halved(x):
        return x >= n // 2 or (x % 2 == 1 and x != 1)

    def w_rows(x, half):
        start = flip(me, x) * channels
        if half:
            return pl.ds(pl.multiple_of(start + group * share, CH), share)
        return pl.ds(pl.multiple_of(start, CH), channels)

    def w_move(x, d):
        half = halved(x + d)
        rows = w_rows(x, half)
        if x:
            src = weight.at[rows]
        elif half:
            src = w_ref.at[pl.ds(pl.multiple_of(group * share, CH), share)]
        else:
            src = w_ref
        return pltpu.make_async_remote_copy(
            src_ref=src,
            dst_ref=weight.at[rows],
            send_sem=w_send.at[x + d],
            recv_sem=w_recv.at[x + d],
            device_id={"swap": flip(me, d)},
            device_id_type=MESH,
        )

    def w_cross(x):
        rows = w_rows(x, True)
        return pltpu.make_async_remote_copy(
            src_ref=weight.at[rows],
            dst_ref=weight.at[rows],
            send_sem=y_send.at[x],
            recv_sem=y_recv.at[x],
            device_id={"group": 1 - group},
            device_id_type=MESH,
        )

    def w_came(x):
        rows = w_rows(x, halved(x))
        return pltpu.make_async_remote_copy(
            src_ref=weight.at[rows],
            dst_ref=weight.at[rows],
            send_sem=w_send.at[x],
            recv_sem=w_recv.at[x],
            device_id={"swap": flip(me, low_bit(x))},
            device_id_type=MESH,
        )

    def pass_on(x):
        w_came(x).wait_recv()
        for d in lower(x, n):
            w_move(x, d).start()
        if halved(x):
            w_cross(x).start()

    def w_own():
        return pltpu.make_async_copy(w_ref, weight.at[w_rows(0, False)], w_own_sem)

    def early(q, i, k):
        peer = flip(me, k)
        return pltpu.make_async_remote_copy(
            src_ref=stage.at[i, peer, pl.ds(pl.multiple_of(q * quarter, CH), quarter)],
            dst_ref=conv.at[i, pl.ds(pl.multiple_of(me * channels + q * quarter, CH), quarter)],
            send_sem=early_send.at[q, i, k],
            recv_sem=early_recv.at[q, i, k],
            device_id={"swap": peer},
            device_id_type=MESH,
        )

    my_rows = pl.ds(pl.multiple_of(me * channels, CH), channels)

    def late(i, k):
        peer = flip(me, k)
        return pltpu.make_async_remote_copy(
            src_ref=stage.at[i, peer],
            dst_ref=conv.at[i, my_rows],
            send_sem=late_send.at[i, k],
            recv_sem=late_recv.at[i, k],
            device_id={"swap": peer},
            device_id_type=MESH,
        )

    def own(i):
        return pltpu.make_async_copy(stage.at[i, me], conv.at[i, my_rows], own_sem.at[i])

    def forward(i):
        return pltpu.make_async_remote_copy(
            src_ref=tok.at[lax.rem(i, 2)],
            dst_ref=tok.at[2 + i],
            send_sem=f_send.at[i],
            recv_sem=f_recv.at[i],
            device_id={"image": other},
            device_id_type=MESH,
        )

    early_hops = [k for k in range(n - 1, 0, -1) if k % 2 == 0]
    late_hops = [k for k in range(n - 1, 0, -1) if k % 2 == 1]
    for d in lower(0, n):
        w_move(0, d).start()
    w_own().start()
    cot_load(0).start()
    cot_load(1).start()
    order = sorted(range(2, n), key=lambda x: (bin(x).count("1"), -x))
    during = (8, 9, 11)

    def chunk(q, carry):
        x_load(q).wait()
        rows = pl.multiple_of(q * CH, CH)
        per = piece // LANES

        def put(i, g, values):
            at = (g % per) * LANES
            stage[i, g // per, pl.ds(rows, CH), at : at + LANES] = values

        conv_chunk(xb.at[lax.rem(q, 2)], rows, u, mask_ref, bias_ref, xf, yf, put)

        @pl.when(q + 2 < chunks)
        def _():
            x_load(q + 2).start()

        for at, x in zip(during, order):

            @pl.when(q == at)
            def _():
                pass_on(x)

        per_quarter = chunks // QUARTERS

        @pl.when(lax.rem(q, per_quarter) == per_quarter - 1)
        def _():
            for i in range(images):
                for k in early_hops:
                    early(q // per_quarter, i, k).start()

        return carry

    lax.fori_loop(0, chunks, chunk, 0)
    for i in range(images):
        own(i).start()
    for j, x in enumerate(order[len(during) :]):
        pass_on(x)
    for i in range(images):
        for k in late_hops:
            late(i, k).start()
    w_came(1).wait_recv()
    for x in range(1, n):
        if halved(x):
            w_cross(x).wait_recv()
    w_own().wait()

    rank = b_ref.shape[0]

    def normalise(i):
        for s in range(piece // LANES):
            at = slice(s * LANES, (s + 1) * LANES)
            x = conv[i, :, at].astype(jnp.float32)
            average = jnp.sum(x, axis=0, keepdims=True) * (1.0 / depth)
            centred = x - average
            variance = jnp.sum(centred * centred, axis=0, keepdims=True) * (1.0 / depth)
            scaled = centred * lax.rsqrt(variance + norm_eps) * gain_ref[...] + shift_ref[...]
            tok[lax.rem(i, 2), at, :] = jnp.swapaxes(scaled, 0, 1).astype(jnp.bfloat16)

    def unit(v, carry):
        i = v // 2
        second = lax.rem(v, 2)

        @pl.when(second == 0)
        def _():
            @pl.when(i >= 2)
            def _():
                forward(i - 2).wait_send()

            own(i).wait()
            for k in early_hops:
                for q in range(QUARTERS):
                    early(q, i, k).wait_recv()
            for k in late_hops:
                late(i, k).wait_recv()
            normalise(i)
            forward(i).start()

        @pl.when(second == 1)
        def _():
            forward(i).wait_recv()

        cot_load(v).wait()
        slot = second * (2 + i) + (1 - second) * lax.rem(i, 2)
        tokens = tok[slot]
        low = jnp.dot(tokens, a_ref[...], preferred_element_type=jnp.float32).astype(jnp.bfloat16)
        wide = low.astype(jnp.float32)
        low_t = jnp.swapaxes(wide, 0, 1).astype(jnp.bfloat16)
        joined = jnp.concatenate([tokens, (adapter_scale * wide).astype(jnp.bfloat16)], axis=1)
        for j in range(hidden // STEP):
            at = slice(j * STEP, (j + 1) * STEP)
            pre = jnp.dot(joined, weight[:, at], preferred_element_type=jnp.float32)
            grad = cot[second, :, at].astype(jnp.float32) * gelu_slope(pre)
            grads[:, at] = grad.astype(jnp.bfloat16)
        grad = grads[...]
        back = lax.dot_general(
            b_ref[...], grad, (((1,), (1,)), ((), ())), preferred_element_type=jnp.float32
        )
        gb_ref[...] += adapter_scale * jnp.dot(low_t, grad, preferred_element_type=jnp.float32)
        high = back.astype(jnp.bfloat16)
        rest = back - high.astype(jnp.float32)
        middle = rest.astype(jnp.bfloat16)
        least = (rest - middle.astype(jnp.float32)).astype(jnp.bfloat16)
        three = jnp.dot(
            jnp.concatenate([high, middle, least], axis=0),
            tokens,
            preferred_element_type=jnp.float32,
        )
        ga_ref[...] += adapter_scale * (
            three[:rank] + three[rank : 2 * rank] + three[2 * rank :]
        )

        @pl.when(v + 2 < 2 * images)
        def _():
            cot_load(v + 2).start()

        return carry

    lax.fori_loop(0, 2 * images, unit, 0)
    sum_grads(n, ga_ref, gb_ref, oa_ref, ob_ref, pair, held, parts, total, pair_sem, s1, r1, s2, r2)
    for i in range(images):
        for k in early_hops:
            for q in range(QUARTERS):
                early(q, i, k).wait_send()
        for k in late_hops:
            late(i, k).wait_send()
    for i in range(max(images - 2, 0), images):
        forward(i).wait_send()
    for x in range(n):
        for d in lower(x, n):
            w_move(x, d).wait_send()
        if halved(x):
            w_cross(x).wait_send()


def sum_grads(n, ga_ref, gb_ref, oa_ref, ob_ref, pair, held, parts, total, pair_sem, s1, r1, s2, r2):
    me = lax.axis_index("swap")
    other = 1 - lax.axis_index("image")
    rank, wide_a = ga_ref.shape
    wide_b = gb_ref.shape[1]
    per = n // (rank // 8)
    ca, cb = wide_a // per, wide_b // per
    swap_a = pltpu.make_async_remote_copy(
        src_ref=ga_ref,
        dst_ref=pair,
        send_sem=pair_sem.at[0],
        recv_sem=pair_sem.at[1],
        device_id={"image": other},
        device_id_type=MESH,
    )
    swap_a.start()

    def place(ref, j, width):
        return ref.at[
            pl.ds(pl.multiple_of((j // per) * 8, 8), 8),
            pl.ds(pl.multiple_of((j % per) * width, 128), width),
        ]

    def move(src, dst, peer, ss, rs):
        return pltpu.make_async_remote_copy(
            src_ref=src,
            dst_ref=dst,
            send_sem=ss,
            recv_sem=rs,
            device_id={"swap": peer},
            device_id_type=MESH,
        )

    def scatter_b(k):
        peer = lax.rem(me + k, n)
        return move(
            place(gb_ref, peer, cb), parts.at[k, :, ca : ca + cb], peer, s1.at[1, k], r1.at[1, k]
        )

    def scatter_a(k):
        peer = lax.rem(me + k, n)
        return move(
            place(held, peer, ca), parts.at[k, :, 0:ca], peer, s1.at[0, k], r1.at[0, k]
        )

    for k in range(1, n):
        scatter_b(k).start()
    swap_a.wait()
    held[...] = ga_ref[...] + pair[...]
    for k in range(1, n):
        scatter_a(k).start()
    sum_b = place(gb_ref, me, cb)[...]
    for k in range(1, n):
        scatter_b(k).wait_recv()
        sum_b = sum_b + parts[k, :, ca : ca + cb]
    sum_a = place(held, me, ca)[...]
    for k in range(1, n):
        scatter_a(k).wait_recv()
        sum_a = sum_a + parts[k, :, 0:ca]
    total[:, 0:ca] = sum_a
    total[:, ca : ca + cb] = sum_b
    place(oa_ref, me, ca)[...] = sum_a
    place(ob_ref, me, cb)[...] = sum_b

    def gather_a(k):
        peer = lax.rem(me + k, n)
        return move(total.at[:, 0:ca], place(oa_ref, me, ca), peer, s2.at[0, k], r2.at[0, k])

    def gather_b(k):
        peer = lax.rem(me + k, n)
        return move(
            total.at[:, ca : ca + cb], place(ob_ref, me, cb), peer, s2.at[1, k], r2.at[1, k]
        )

    for k in range(1, n):
        gather_b(k).start()
        gather_a(k).start()
    for k in range(1, n):
        gather_b(k).wait_recv()
        gather_a(k).wait_recv()
    for k in range(1, n):
        scatter_a(k).wait_send()
        scatter_b(k).wait_send()
        gather_a(k).wait_send()
        gather_b(k).wait_send()


def fused(n, images_in, kernel, conv_bias, weight, cotangent, adapter_a, adapter_b, gain, shift):
    images, channels, pixels = images_in.shape
    piece = pixels // n
    hidden = weight.shape[1]
    rank = adapter_b.shape[0]
    depth = channels * n
    pairs = pixels // LANES
    per = n // (rank // 8)
    wide = depth // per + hidden // per
    dma = pltpu.SemaphoreType.DMA
    vmem = pl.BlockSpec(memory_space=pltpu.VMEM)
    hbm = pl.BlockSpec(memory_space=pltpu.HBM)
    bf16, f32 = jnp.bfloat16, jnp.float32
    return pl.pallas_call(
        functools.partial(fused_kernel, n),
        out_shape=(
            jax.ShapeDtypeStruct((rank, depth), f32),
            jax.ShapeDtypeStruct((rank, hidden), f32),
        ),
        in_specs=[hbm, vmem, vmem, vmem, vmem, vmem, hbm, vmem, vmem, vmem, vmem],
        out_specs=(vmem, vmem),
        scratch_shapes=[
            pltpu.VMEM((2, images, CH, pixels), bf16),
            pltpu.VMEM((KS + 1, channels, LANES), f32),
            pltpu.VMEM((images * (pairs + 3) * CH, LANES), f32),
            pltpu.VMEM((images * pairs * CH, LANES), f32),
            pltpu.VMEM((images, n, channels, piece), bf16),
            pltpu.VMEM((images, depth, piece), bf16),
            pltpu.VMEM((depth + rank, hidden), bf16),
            pltpu.VMEM((2, piece, hidden), bf16),
            pltpu.VMEM((2 + images, piece, depth), bf16),
            pltpu.VMEM((piece, hidden), bf16),
            pltpu.VMEM((rank, depth), f32),
            pltpu.VMEM((rank, hidden), f32),
            pltpu.VMEM((rank, depth), f32),
            pltpu.VMEM((rank, depth), f32),
            pltpu.VMEM((n, 8, wide), f32),
            pltpu.VMEM((8, wide), f32),
            dma((2,)),
            dma((2,)),
            dma((images,)),
            dma,
            dma((QUARTERS, images, n)),
            dma((QUARTERS, images, n)),
            dma((images, n)),
            dma((images, n)),
            dma((n,)),
            dma((n,)),
            dma((n,)),
            dma((n,)),
            dma((images,)),
            dma((images,)),
            dma((2,)),
            dma((2, n)),
            dma((2, n)),
            dma((2, n)),
            dma((2, n)),
        ],
        compiler_params=pltpu.CompilerParams(
            collective_id=0, has_side_effects=True, vmem_limit_bytes=62 * 2**20
        ),
        name="fused",
    )(
        images_in,
        kernel,
        conv_bias[:, None],
        jnp.asarray(band_table(), bf16),
        jnp.asarray(band_mask()),
        weight,
        cotangent,
        adapter_a,
        adapter_b,
        gain[:, None],
        shift[:, None],
    )


def fast_shards(
    n,
    images_in,
    kernel,
    conv_bias,
    norm_gain,
    norm_shift,
    fp8_weight,
    block_scale,
    adapter_a,
    adapter_b,
    cotangent,
):
    grad_a, grad_b = fused(
        n,
        images_in,
        kernel,
        conv_bias,
        decode(fp8_weight, block_scale),
        cotangent,
        adapter_a,
        adapter_b,
        norm_gain,
        norm_shift,
    )
    return (grad_a.T, grad_b)


def fits(n, images_in, fp8_weight, adapter_a):
    images, channels, pixels = images_in.shape
    rank = adapter_a.shape[1]
    piece = pixels // n
    per = n // (rank // 8) if rank % 8 == 0 else 0
    wide = fp8_weight.shape[1]
    return (
        per > 0
        and n >= 4
        and n & (n - 1) == 0
        and n % (rank // 8) == 0
        and rank % 16 == 0
        and channels % (2 * CH) == 0
        and channels % (QUARTERS * CH) == 0
        and pixels % n == 0
        and piece % LANES == 0
        and wide % STEP == 0
        and (channels * n) % (per * 128) == 0
        and wide % (per * 128) == 0
    )


def depthwise(images, kernel, conv_bias, map_width):
    batch, channels, pixels = images.shape
    maps = images.reshape(batch, channels, pixels // map_width, map_width)
    taps = kernel.reshape(channels, 1, KS, KS)
    half_span = KS // 2
    summed = lax.conv_general_dilated(
        maps,
        taps,
        (1, 1),
        ((half_span, half_span), (half_span, half_span)),
        dimension_numbers=("NCHW", "OIHW", "NCHW"),
        feature_group_count=channels,
        preferred_element_type=jnp.float32,
    )
    summed = summed.reshape(batch, channels, pixels)
    return summed + conv_bias[None, :, None]


def plain_shards(
    images_in,
    kernel,
    conv_bias,
    norm_gain,
    norm_shift,
    fp8_weight,
    block_scale,
    adapter_a,
    adapter_b,
    cotangent,
):
    conv = depthwise(images_in, kernel, conv_bias, W).astype(jnp.bfloat16)
    values = lax.all_to_all(conv, "swap", split_axis=2, concat_axis=1, tiled=True).astype(
        jnp.float32
    )
    average = jnp.mean(values, axis=1, keepdims=True)
    centred = values - average
    variance = jnp.mean(centred * centred, axis=1, keepdims=True)
    scaled = (
        centred * lax.rsqrt(variance + norm_eps) * norm_gain[None, :, None]
        + norm_shift[None, :, None]
    )
    normed = jnp.swapaxes(scaled, 1, 2).astype(jnp.bfloat16)
    own_rows = normed.reshape(-1, normed.shape[2])
    tokens = lax.all_gather(own_rows, "image", axis=0, tiled=True)
    zero_start = jnp.zeros((tokens.shape[0], fp8_weight.shape[1]), jnp.float32)
    local_weight = decode(fp8_weight, block_scale)
    shard_rows = lax.all_gather(local_weight, "swap", axis=0, tiled=True)
    columns = lax.slice_in_dim(tokens, 0, shard_rows.shape[0], axis=1)
    frozen = zero_start + jnp.dot(columns, shard_rows, preferred_element_type=jnp.float32)
    low_rank = jnp.dot(tokens, adapter_a, preferred_element_type=jnp.float32).astype(jnp.bfloat16)
    pre_act = frozen + adapter_scale * jnp.dot(
        low_rank, adapter_b, preferred_element_type=jnp.float32
    )
    upstream = cotangent.reshape(-1, cotangent.shape[2])
    grad_pre = (upstream.astype(jnp.float32) * gelu_slope(pre_act)).astype(jnp.bfloat16)
    grad_b_local = adapter_scale * jnp.dot(low_rank.T, grad_pre, preferred_element_type=jnp.float32)
    partial_back = jnp.dot(grad_pre, adapter_b.T, preferred_element_type=jnp.float32)
    contract = (((0,), (0,)), ((), ()))
    tokens_wide = tokens.astype(jnp.float32)
    summed_back = lax.psum(partial_back, "image")
    grad_a_local = adapter_scale * lax.dot_general(
        tokens_wide,
        summed_back,
        contract,
        precision=lax.Precision.HIGHEST,
        preferred_element_type=jnp.float32,
    )
    grad_a, grad_b = lax.psum((grad_a_local, grad_b_local), "swap")
    return (grad_a, grad_b)


def solution(mesh):
    placed = (
        P(("group", "image"), "swap", None),
        P("swap", None),
        P("swap"),
        P(),
        P(),
        P("swap", "image"),
        P("swap", "image"),
        P(),
        P(None, "image"),
        P("group", "swap", "image"),
    )
    n = mesh.shape["swap"]

    def shards(*arrays):
        if mesh.shape["image"] == 2 and mesh.shape["group"] == 2 and fits(n, arrays[0], arrays[5], arrays[7]):
            return fast_shards(n, *arrays)
        return plain_shards(*arrays)

    return jax.shard_map(
        shards,
        mesh=mesh,
        in_specs=placed,
        out_specs=(P("group", None), P("group", "image")),
        check_vma=False,
    )
```

```python
import functools

import jax
import jax.numpy as jnp
import numpy as np
from jax import lax
from jax.experimental import pallas as pl
from jax.experimental.pallas import tpu as pltpu
from jax.sharding import PartitionSpec as P

KS = 7
W = 64
HALF = KS // 2
MESH = pl.DeviceIdType.MESH
CH = 16
LANES = 2 * W
QUARTERS = 4
STEP = 512


adapter_scale = 2.0
norm_eps = 1e-06


def power_table(scales):
    factor = jnp.zeros(scales.shape, jnp.float32)
    for exponent in range(-12, 4):
        factor = factor + jnp.where(
            scales == exponent, jnp.float32(2.0**exponent), jnp.float32(0.0)
        )
    return factor


def decode(weight, scales):
    row_count = weight.shape[0]
    groups = scales.shape[1]
    blocks = (
        weight.reshape(row_count, groups, -1).astype(jnp.float32) * power_table(scales)[:, :, None]
    )
    return blocks.reshape(row_count, -1).astype(jnp.bfloat16)


def gelu_slope(pre_act):
    cumulative = 0.5 * (1.0 + lax.erf(pre_act * 0.7071067811865476))
    density = jnp.exp(-0.5 * pre_act * pre_act) * 0.3989422804014327
    return cumulative + pre_act * density


def band_table():
    table = np.zeros((KS * KS, (KS + 1) * LANES), np.float32)
    for s in range(KS + 1):
        for r in range(2):
            a = s - r
            if 0 <= a < KS:
                for b in range(KS):
                    table[a * KS + b, s * LANES + (r * W + HALF - b) % LANES] = 1.0
    return table


def band_mask():
    rows = np.arange(W)[:, None]
    lanes = np.arange(LANES)[None, :] % W
    return (np.abs(rows - lanes) <= HALF).astype(np.float32)


def flip(me, bits):
    out = me
    d = 1
    while d <= bits:
        if bits & d:
            out = out + d - 2 * d * lax.rem(me // d, 2)
        d *= 2
    return out


def conv_chunk(xb, rows, u, mask_ref, bias_ref, xf, yf, put):
    images, ch, pixels = xb.shape
    pairs = pixels // LANES
    span = pairs + 3
    for i in range(images):
        x = xb[i].astype(jnp.float32)
        x = jnp.concatenate([x, jnp.zeros((ch, LANES), jnp.float32)], axis=1)
        x = pltpu.roll(x, W, axis=1)
        for g in range(pairs + 1):
            xf[pl.ds((i * span + g + 1) * ch, ch), :] = x[:, g * LANES : (g + 1) * LANES]
    mask = mask_ref[...]
    for c in range(ch):
        bands = []
        for s in range(KS + 1):
            first = jnp.broadcast_to(u[s, pl.ds(rows + c, 1), :], (W, LANES))
            band = pltpu.roll(first, 0, 1, stride=1, stride_axis=0) * mask
            bands.append(band.astype(jnp.bfloat16))
        parts = []
        for i in range(images):
            moved = [
                xf[pl.ds((i * span + j) * ch + c, pairs, stride=ch), :].astype(jnp.bfloat16)
                for j in range((KS + 1) // 2)
            ]
            parts.append(jnp.concatenate(moved, axis=1))
        y = jnp.dot(
            jnp.concatenate(parts, axis=0),
            jnp.concatenate(bands, axis=0),
            preferred_element_type=jnp.float32,
        )
        yf[pl.ds(c, images * pairs, stride=ch), :] = y + bias_ref[rows + c]
    for i in range(images):
        for g in range(pairs):
            put(i, g, yf[pl.ds((i * pairs + g) * ch, ch), :].astype(jnp.bfloat16))


def low_bit(x):
    return x & -x


def lower(x, n):
    hops = []
    d = (low_bit(x) if x else n) // 2
    while d >= 1:
        hops.append(d)
        d //= 2
    return hops


def fused_kernel(
    n,
    x_hbm,
    k_ref,
    bias_ref,
    table_ref,
    mask_ref,
    w_ref,
    scale_ref,
    cot_hbm,
    a_ref,
    b_ref,
    gain_ref,
    shift_ref,
    oa_ref,
    ob_ref,
    xb,
    u,
    xf,
    yf,
    stage,
    conv,
    weight,
    cot,
    tok,
    grads,
    ga_ref,
    gb_ref,
    pair,
    held,
    parts,
    total,
    x_sem,
    cot_sem,
    own_sem,
    early_send,
    early_recv,
    late_send,
    late_recv,
    w_send,
    w_recv,
    y_send,
    y_recv,
    f_send,
    f_recv,
    pair_sem,
    s1,
    r1,
    s2,
    r2,
):
    images, channels, pixels = x_hbm.shape
    piece = pixels // n
    hidden = w_ref.shape[1]
    depth = channels * n
    chunks = channels // CH
    quarter = channels // QUARTERS
    me = lax.axis_index("swap")
    core = lax.axis_index("image")
    other = 1 - core
    group = lax.axis_index("group")

    def x_load(q):
        slot = lax.rem(q, 2)
        return pltpu.make_async_copy(
            x_hbm.at[:, pl.ds(pl.multiple_of(q * CH, CH), CH), :], xb.at[slot], x_sem.at[slot]
        )

    def cot_load(unit):
        slot = lax.rem(unit, 2)
        image = lax.rem(core + lax.rem(unit, 2), 2) * images + unit // 2
        return pltpu.make_async_copy(cot_hbm.at[image], cot.at[slot], cot_sem.at[slot])

    x_load(0).start()
    x_load(1).start()
    barrier = pltpu.get_barrier_semaphore()
    for k in range(1, n):
        pl.semaphore_signal(
            barrier, inc=1, device_id={"swap": flip(me, k)}, device_id_type=MESH
        )
    pl.semaphore_signal(barrier, inc=1, device_id={"image": other}, device_id_type=MESH)
    pl.semaphore_signal(barrier, inc=1, device_id={"group": 1 - group}, device_id_type=MESH)

    groups = scale_ref.shape[0]
    size = hidden // groups
    my_rows = pl.ds(pl.multiple_of(me * channels, CH), channels)
    factor = power_table(scale_ref[...]).astype(jnp.bfloat16)
    for j in range(hidden // STEP):
        at = slice(j * STEP, (j + 1) * STEP)
        block = lax.broadcasted_iota(jnp.int32, (groups, STEP), 1) + j * STEP
        first = lax.broadcasted_iota(jnp.int32, (groups, STEP), 0) * size
        spread = jnp.where((block >= first) & (block < first + size), 1.0, 0.0)
        wide = lax.dot_general(
            factor,
            spread.astype(jnp.bfloat16),
            (((0,), (0,)), ((), ())),
            preferred_element_type=jnp.float32,
        )
        weight[my_rows, at] = (w_ref[:, at].astype(jnp.float32) * wide).astype(jnp.bfloat16)
    zero = jnp.zeros((CH, LANES), jnp.float32)
    span = pixels // LANES + 3
    for i in range(images):
        xf[pl.ds(i * span * CH, CH), :] = zero
        xf[pl.ds((i * span + span - 1) * CH, CH), :] = zero
    for s in range(KS + 1):
        u[s] = lax.dot_general(
            k_ref[...],
            table_ref[:, s * LANES : (s + 1) * LANES],
            (((0,), (0,)), ((), ())),
            preferred_element_type=jnp.float32,
        )
    ga_ref[...] = jnp.zeros_like(ga_ref)
    gb_ref[...] = jnp.zeros_like(gb_ref)
    weight[depth:, :] = b_ref[...]
    pl.semaphore_wait(barrier, n + 1)

    share = channels // 2

    def halved(x):
        return x >= n // 2 or (x % 2 == 1 and x != 1)

    bit = share // 2

    def pieces(x):
        return (0, 1) if halved(x) else (0, 1, 2)

    def w_piece(p):
        if p == 2:
            return (1 - group) * share, share
        return group * share + p * bit, bit

    def w_rows(x, p):
        start, count = w_piece(p)
        return pl.ds(pl.multiple_of(flip(me, x) * channels + start, CH), count)

    def w_move(x, d, p):
        rows = w_rows(x, p)
        return pltpu.make_async_remote_copy(
            src_ref=weight.at[rows],
            dst_ref=weight.at[rows],
            send_sem=w_send.at[x + d, p],
            recv_sem=w_recv.at[x + d, p],
            device_id={"swap": flip(me, d)},
            device_id_type=MESH,
        )

    def w_cross(x, p):
        rows = w_rows(x, p)
        return pltpu.make_async_remote_copy(
            src_ref=weight.at[rows],
            dst_ref=weight.at[rows],
            send_sem=y_send.at[x, p],
            recv_sem=y_recv.at[x, p],
            device_id={"group": 1 - group},
            device_id_type=MESH,
        )

    def w_crossed(x, p):
        start = flip(me, x) * channels + (1 - group) * share + p * bit
        rows = pl.ds(pl.multiple_of(start, CH), bit)
        return pltpu.make_async_remote_copy(
            src_ref=weight.at[rows],
            dst_ref=weight.at[rows],
            send_sem=y_send.at[x, p],
            recv_sem=y_recv.at[x, p],
            device_id={"group": 1 - group},
            device_id_type=MESH,
        )

    def w_came(x, p):
        rows = w_rows(x, p)
        return pltpu.make_async_remote_copy(
            src_ref=weight.at[rows],
            dst_ref=weight.at[rows],
            send_sem=w_send.at[x, p],
            recv_sem=w_recv.at[x, p],
            device_id={"swap": flip(me, low_bit(x))},
            device_id_type=MESH,
        )

    def passed(x, p):
        return [d for d in lower(x, n) if p in pieces(x + d)]

    def pass_on(x, p):
        w_came(x, p).wait_recv()
        for d in passed(x, p):
            w_move(x, d, p).start()
        if halved(x):
            w_cross(x, p).start()

    def early(q, i, k):
        peer = flip(me, k)
        return pltpu.make_async_remote_copy(
            src_ref=stage.at[i, peer, pl.ds(pl.multiple_of(q * quarter, CH), quarter)],
            dst_ref=conv.at[i, pl.ds(pl.multiple_of(me * channels + q * quarter, CH), quarter)],
            send_sem=early_send.at[q, i, k],
            recv_sem=early_recv.at[q, i, k],
            device_id={"swap": peer},
            device_id_type=MESH,
        )

    def late(i, k):
        peer = flip(me, k)
        return pltpu.make_async_remote_copy(
            src_ref=stage.at[i, peer],
            dst_ref=conv.at[i, my_rows],
            send_sem=late_send.at[i, k],
            recv_sem=late_recv.at[i, k],
            device_id={"swap": peer},
            device_id_type=MESH,
        )

    def own(i):
        return pltpu.make_async_copy(stage.at[i, me], conv.at[i, my_rows], own_sem.at[i])

    def forward(i):
        return pltpu.make_async_remote_copy(
            src_ref=tok.at[lax.rem(i, 2)],
            dst_ref=tok.at[2 + i],
            send_sem=f_send.at[i],
            recv_sem=f_recv.at[i],
            device_id={"image": other},
            device_id_type=MESH,
        )

    early_hops = [4,6]
    late_hops = [5,7,2,1,3]
    for d in lower(0, n):
        for p in pieces(d):
            w_move(0, d, p).start()
    cot_load(0).start()
    cot_load(1).start()
    order = sorted(range(2, n), key=lambda x: (bin(x).count("1"), -x))
    order = [(x, p) for x in order for p in pieces(x) if halved(x) or passed(x, p)]
    during = (2, 5, 8, 9, 10, 11)

    def chunk(q, carry):
        x_load(q).wait()
        rows = pl.multiple_of(q * CH, CH)
        per = piece // LANES

        def put(i, g, values):
            at = (g % per) * LANES
            stage[i, g // per, pl.ds(rows, CH), at : at + LANES] = values

        conv_chunk(xb.at[lax.rem(q, 2)], rows, u, mask_ref, bias_ref, xf, yf, put)

        @pl.when(q + 2 < chunks)
        def _():
            x_load(q + 2).start()

        for at, (x, p) in zip(during, order):

            @pl.when(q == at)
            def _():
                pass_on(x, p)

        per_quarter = chunks // QUARTERS

        @pl.when(lax.rem(q, per_quarter) == per_quarter - 1)
        def _():
            for i in range(3):
                for k in early_hops:
                    early(q // per_quarter, i, k).start()

        return carry

    lax.fori_loop(0, chunks, chunk, 0)
    for i in range(images):
        own(i).start()
    for x, p in order[len(during) :]:
        pass_on(x, p)
    for i in range(images):
        for k in late_hops:
            late(i, k).start()
        if i >= 3:
            for q in range(QUARTERS):
                for k in early_hops:
                    early(q, i, k).start()
    for x in range(1, n):
        if halved(x):
            for p in pieces(x):
                w_crossed(x, p).wait_recv()
        else:
            for p in pieces(x):
                if not passed(x, p):
                    w_came(x, p).wait_recv()

    rank = b_ref.shape[0]

    def normalise(i):
        for s in range(piece // LANES):
            at = slice(s * LANES, (s + 1) * LANES)
            x = conv[i, :, at].astype(jnp.float32)
            average = jnp.sum(x, axis=0, keepdims=True) * (1.0 / depth)
            centred = x - average
            variance = jnp.sum(centred * centred, axis=0, keepdims=True) * (1.0 / depth)
            scaled = jnp.swapaxes(centred * lax.rsqrt(variance + norm_eps), 0, 1)
            scaled = scaled * gain_ref[...][None, :] + shift_ref[...][None, :]
            tok[lax.rem(i, 2), at, :] = scaled.astype(jnp.bfloat16)

    def unit(v, carry):
        i = v // 2
        second = lax.rem(v, 2)

        @pl.when(second == 0)
        def _():
            @pl.when(i >= 2)
            def _():
                forward(i - 2).wait_send()

            own(i).wait()
            for k in early_hops:
                for q in range(QUARTERS):
                    early(q, i, k).wait_recv()
            for k in late_hops:
                late(i, k).wait_recv()
            normalise(i)
            forward(i).start()

        @pl.when(second == 1)
        def _():
            forward(i).wait_recv()

        cot_load(v).wait()
        slot = second * (2 + i) + (1 - second) * lax.rem(i, 2)
        tokens = tok[slot]
        low = lax.dot_general(
            tokens, a_ref[...], (((1,), (1,)), ((), ())), preferred_element_type=jnp.float32
        ).astype(jnp.bfloat16)
        wide = low.astype(jnp.float32)
        low_t = jnp.swapaxes(wide, 0, 1).astype(jnp.bfloat16)
        joined = jnp.concatenate([tokens, (adapter_scale * wide).astype(jnp.bfloat16)], axis=1)
        for j in range(hidden // STEP):
            at = slice(j * STEP, (j + 1) * STEP)
            pre = jnp.dot(joined, weight[:, at], preferred_element_type=jnp.float32)
            grad = cot[second, :, at].astype(jnp.float32) * gelu_slope(pre)
            grads[:, at] = grad.astype(jnp.bfloat16)
        grad = grads[...]
        back = lax.dot_general(
            b_ref[...], grad, (((1,), (1,)), ((), ())), preferred_element_type=jnp.float32
        )
        gb_ref[...] += adapter_scale * jnp.dot(low_t, grad, preferred_element_type=jnp.float32)
        high = back.astype(jnp.bfloat16)
        rest = back - high.astype(jnp.float32)
        middle = rest.astype(jnp.bfloat16)
        least = (rest - middle.astype(jnp.float32)).astype(jnp.bfloat16)
        three = jnp.dot(
            jnp.concatenate([high, middle, least], axis=0),
            tokens,
            preferred_element_type=jnp.float32,
        )
        ga_ref[...] += adapter_scale * (
            three[:rank] + three[rank : 2 * rank] + three[2 * rank :]
        )

        @pl.when(v + 2 < 2 * images)
        def _():
            cot_load(v + 2).start()

        return carry

    lax.fori_loop(0, 2 * images, unit, 0)
    sum_grads(n, ga_ref, gb_ref, oa_ref, ob_ref, pair, held, parts, total, pair_sem, s1, r1, s2, r2)
    for i in range(images):
        for k in early_hops:
            for q in range(QUARTERS):
                early(q, i, k).wait_send()
        for k in late_hops:
            late(i, k).wait_send()
    for i in range(max(images - 2, 0), images):
        forward(i).wait_send()
    for x in range(n):
        for d in lower(x, n):
            for p in pieces(x + d):
                w_move(x, d, p).wait_send()
        if halved(x):
            for p in pieces(x):
                w_cross(x, p).wait_send()


def sum_grads(n, ga_ref, gb_ref, oa_ref, ob_ref, pair, held, parts, total, pair_sem, s1, r1, s2, r2):
    me = lax.axis_index("swap")
    other = 1 - lax.axis_index("image")
    rank, wide_a = ga_ref.shape
    wide_b = gb_ref.shape[1]
    per = n // (rank // 8)
    ca, cb = wide_a // per, wide_b // per
    swap_a = pltpu.make_async_remote_copy(
        src_ref=ga_ref,
        dst_ref=pair,
        send_sem=pair_sem.at[0],
        recv_sem=pair_sem.at[1],
        device_id={"image": other},
        device_id_type=MESH,
    )
    swap_a.start()

    def place(ref, j, width):
        return ref.at[
            pl.ds(pl.multiple_of((j // per) * 8, 8), 8),
            pl.ds(pl.multiple_of((j % per) * width, 128), width),
        ]

    def move(src, dst, peer, ss, rs):
        return pltpu.make_async_remote_copy(
            src_ref=src,
            dst_ref=dst,
            send_sem=ss,
            recv_sem=rs,
            device_id={"swap": peer},
            device_id_type=MESH,
        )

    def scatter_b(k):
        peer = lax.rem(me + k, n)
        return move(
            place(gb_ref, peer, cb), parts.at[k, :, ca : ca + cb], peer, s1.at[1, k], r1.at[1, k]
        )

    def scatter_a(k):
        peer = lax.rem(me + k, n)
        return move(
            place(held, peer, ca), parts.at[k, :, 0:ca], peer, s1.at[0, k], r1.at[0, k]
        )

    for k in range(1, n):
        scatter_b(k).start()
    swap_a.wait()
    held[...] = ga_ref[...] + pair[...]
    for k in range(1, n):
        scatter_a(k).start()
    sum_b = place(gb_ref, me, cb)[...]
    for k in range(1, n):
        scatter_b(k).wait_recv()
        sum_b = sum_b + parts[k, :, ca : ca + cb]
    sum_a = place(held, me, ca)[...]
    for k in range(1, n):
        scatter_a(k).wait_recv()
        sum_a = sum_a + parts[k, :, 0:ca]
    total[:, 0:ca] = sum_a
    total[:, ca : ca + cb] = sum_b
    place(oa_ref, me, ca)[...] = sum_a
    place(ob_ref, me, cb)[...] = sum_b

    def gather_a(k):
        peer = lax.rem(me + k, n)
        return move(total.at[:, 0:ca], place(oa_ref, me, ca), peer, s2.at[0, k], r2.at[0, k])

    def gather_b(k):
        peer = lax.rem(me + k, n)
        return move(
            total.at[:, ca : ca + cb], place(ob_ref, me, cb), peer, s2.at[1, k], r2.at[1, k]
        )

    for k in range(1, n):
        gather_b(k).start()
        gather_a(k).start()
    for k in range(1, n):
        gather_b(k).wait_recv()
        gather_a(k).wait_recv()
    for k in range(1, n):
        scatter_a(k).wait_send()
        scatter_b(k).wait_send()
        gather_a(k).wait_send()
        gather_b(k).wait_send()


def fused(
    n, images_in, kernel, conv_bias, weight, scales, cotangent, adapter_a, adapter_b, gain, shift
):
    images, channels, pixels = images_in.shape
    piece = pixels // n
    hidden = weight.shape[1]
    rank = adapter_b.shape[0]
    depth = channels * n
    pairs = pixels // LANES
    per = n // (rank // 8)
    wide = depth // per + hidden // per
    dma = pltpu.SemaphoreType.DMA
    vmem = pl.BlockSpec(memory_space=pltpu.VMEM)
    hbm = pl.BlockSpec(memory_space=pltpu.HBM)
    smem = pl.BlockSpec(memory_space=pltpu.SMEM)
    bf16, f32 = jnp.bfloat16, jnp.float32
    return pl.pallas_call(
        functools.partial(fused_kernel, n),
        out_shape=(
            jax.ShapeDtypeStruct((rank, depth), f32),
            jax.ShapeDtypeStruct((rank, hidden), f32),
        ),
        in_specs=[hbm, vmem, smem, vmem, vmem, vmem, vmem, hbm, vmem, vmem, vmem, vmem],
        out_specs=(vmem, vmem),
        scratch_shapes=[
            pltpu.VMEM((2, images, CH, pixels), bf16),
            pltpu.VMEM((KS + 1, channels, LANES), f32),
            pltpu.VMEM((images * (pairs + 3) * CH, LANES), f32),
            pltpu.VMEM((images * pairs * CH, LANES), f32),
            pltpu.VMEM((images, n, channels, piece), bf16),
            pltpu.VMEM((images, depth, piece), bf16),
            pltpu.VMEM((depth + rank, hidden), bf16),
            pltpu.VMEM((2, piece, hidden), bf16),
            pltpu.VMEM((2 + images, piece, depth), bf16),
            pltpu.VMEM((piece, hidden), bf16),
            pltpu.VMEM((rank, depth), f32),
            pltpu.VMEM((rank, hidden), f32),
            pltpu.VMEM((rank, depth), f32),
            pltpu.VMEM((rank, depth), f32),
            pltpu.VMEM((n, 8, wide), f32),
            pltpu.VMEM((8, wide), f32),
            dma((2,)),
            dma((2,)),
            dma((images,)),
            dma((QUARTERS, images, n)),
            dma((QUARTERS, images, n)),
            dma((images, n)),
            dma((images, n)),
            dma((n, 3)),
            dma((n, 3)),
            dma((n, 2)),
            dma((n, 2)),
            dma((images,)),
            dma((images,)),
            dma((2,)),
            dma((2, n)),
            dma((2, n)),
            dma((2, n)),
            dma((2, n)),
        ],
        compiler_params=pltpu.CompilerParams(
            collective_id=0, has_side_effects=True, vmem_limit_bytes=62 * 2**20
        ),
        name="fused",
    )(
        images_in,
        kernel.T,
        conv_bias,
        jnp.asarray(band_table(), bf16),
        jnp.asarray(band_mask()),
        weight,
        scales.T,
        cotangent,
        adapter_a.T,
        adapter_b,
        gain,
        shift,
    )


def fast_shards(
    n,
    images_in,
    kernel,
    conv_bias,
    norm_gain,
    norm_shift,
    fp8_weight,
    block_scale,
    adapter_a,
    adapter_b,
    cotangent,
):
    grad_a, grad_b = fused(
        n,
        images_in,
        kernel,
        conv_bias,
        fp8_weight,
        block_scale,
        cotangent,
        adapter_a,
        adapter_b,
        norm_gain,
        norm_shift,
    )
    return (grad_a.T, grad_b)


def fits(n, images_in, fp8_weight, adapter_a):
    images, channels, pixels = images_in.shape
    rank = adapter_a.shape[1]
    piece = pixels // n
    per = n // (rank // 8) if rank % 8 == 0 else 0
    wide = fp8_weight.shape[1]
    return (
        per > 0
        and n >= 4
        and n & (n - 1) == 0
        and n % (rank // 8) == 0
        and rank % 16 == 0
        and channels % (2 * CH) == 0
        and channels % (QUARTERS * CH) == 0
        and pixels % n == 0
        and piece % LANES == 0
        and wide % STEP == 0
        and (channels * n) % (per * 128) == 0
        and wide % (per * 128) == 0
    )


def depthwise(images, kernel, conv_bias, map_width):
    batch, channels, pixels = images.shape
    maps = images.reshape(batch, channels, pixels // map_width, map_width)
    taps = kernel.reshape(channels, 1, KS, KS)
    half_span = KS // 2
    summed = lax.conv_general_dilated(
        maps,
        taps,
        (1, 1),
        ((half_span, half_span), (half_span, half_span)),
        dimension_numbers=("NCHW", "OIHW", "NCHW"),
        feature_group_count=channels,
        preferred_element_type=jnp.float32,
    )
    summed = summed.reshape(batch, channels, pixels)
    return summed + conv_bias[None, :, None]


def plain_shards(
    images_in,
    kernel,
    conv_bias,
    norm_gain,
    norm_shift,
    fp8_weight,
    block_scale,
    adapter_a,
    adapter_b,
    cotangent,
):
    conv = depthwise(images_in, kernel, conv_bias, W).astype(jnp.bfloat16)
    values = lax.all_to_all(conv, "swap", split_axis=2, concat_axis=1, tiled=True).astype(
        jnp.float32
    )
    average = jnp.mean(values, axis=1, keepdims=True)
    centred = values - average
    variance = jnp.mean(centred * centred, axis=1, keepdims=True)
    scaled = (
        centred * lax.rsqrt(variance + norm_eps) * norm_gain[None, :, None]
        + norm_shift[None, :, None]
    )
    normed = jnp.swapaxes(scaled, 1, 2).astype(jnp.bfloat16)
    own_rows = normed.reshape(-1, normed.shape[2])
    tokens = lax.all_gather(own_rows, "image", axis=0, tiled=True)
    zero_start = jnp.zeros((tokens.shape[0], fp8_weight.shape[1]), jnp.float32)
    local_weight = decode(fp8_weight, block_scale)
    shard_rows = lax.all_gather(local_weight, "swap", axis=0, tiled=True)
    columns = lax.slice_in_dim(tokens, 0, shard_rows.shape[0], axis=1)
    frozen = zero_start + jnp.dot(columns, shard_rows, preferred_element_type=jnp.float32)
    low_rank = jnp.dot(tokens, adapter_a, preferred_element_type=jnp.float32).astype(jnp.bfloat16)
    pre_act = frozen + adapter_scale * jnp.dot(
        low_rank, adapter_b, preferred_element_type=jnp.float32
    )
    upstream = cotangent.reshape(-1, cotangent.shape[2])
    grad_pre = (upstream.astype(jnp.float32) * gelu_slope(pre_act)).astype(jnp.bfloat16)
    grad_b_local = adapter_scale * jnp.dot(low_rank.T, grad_pre, preferred_element_type=jnp.float32)
    partial_back = jnp.dot(grad_pre, adapter_b.T, preferred_element_type=jnp.float32)
    contract = (((0,), (0,)), ((), ()))
    tokens_wide = tokens.astype(jnp.float32)
    summed_back = lax.psum(partial_back, "image")
    grad_a_local = adapter_scale * lax.dot_general(
        tokens_wide,
        summed_back,
        contract,
        precision=lax.Precision.HIGHEST,
        preferred_element_type=jnp.float32,
    )
    grad_a, grad_b = lax.psum((grad_a_local, grad_b_local), "swap")
    return (grad_a, grad_b)


def solution(mesh):
    placed = (
        P(("group", "image"), "swap", None),
        P("swap", None),
        P("swap"),
        P(),
        P(),
        P("swap", "image"),
        P("swap", "image"),
        P(),
        P(None, "image"),
        P("group", "swap", "image"),
    )
    n = mesh.shape["swap"]

    def shards(*arrays):
        if mesh.shape["image"] == 2 and mesh.shape["group"] == 2 and fits(n, arrays[0], arrays[5], arrays[7]):
            return fast_shards(n, *arrays)
        return plain_shards(*arrays)

    return jax.shard_map(
        shards,
        mesh=mesh,
        in_specs=placed,
        out_specs=(P("group", None), P("group", "image")),
        check_vma=False,
    )
```

```python
import functools

import jax
import jax.numpy as jnp
import numpy as np
from jax import lax
from jax.experimental import pallas as pl
from jax.experimental.pallas import tpu as pltpu
from jax.sharding import PartitionSpec as P

KS = 7
W = 64
HALF = KS // 2
MESH = pl.DeviceIdType.MESH
CH = 16
LANES = 2 * W
QUARTERS = 4
STEP = 512


adapter_scale = 2.0
norm_eps = 1e-06


def power_table(scales):
    factor = jnp.zeros(scales.shape, jnp.float32)
    for exponent in range(-12, 4):
        factor = factor + jnp.where(
            scales == exponent, jnp.float32(2.0**exponent), jnp.float32(0.0)
        )
    return factor


def decode(weight, scales):
    row_count = weight.shape[0]
    groups = scales.shape[1]
    blocks = (
        weight.reshape(row_count, groups, -1).astype(jnp.float32) * power_table(scales)[:, :, None]
    )
    return blocks.reshape(row_count, -1).astype(jnp.bfloat16)


def gelu_slope(pre_act):
    cumulative = 0.5 * (1.0 + lax.erf(pre_act * 0.7071067811865476))
    density = jnp.exp(-0.5 * pre_act * pre_act) * 0.3989422804014327
    return cumulative + pre_act * density


def band_table():
    table = np.zeros((KS * KS, (KS + 1) * LANES), np.float32)
    for s in range(KS + 1):
        for r in range(2):
            a = s - r
            if 0 <= a < KS:
                for b in range(KS):
                    table[a * KS + b, s * LANES + (r * W + HALF - b) % LANES] = 1.0
    return table


def band_mask():
    rows = np.arange(W)[:, None]
    lanes = np.arange(LANES)[None, :] % W
    return (np.abs(rows - lanes) <= HALF).astype(np.float32)


def flip(me, bits):
    out = me
    d = 1
    while d <= bits:
        if bits & d:
            out = out + d - 2 * d * lax.rem(me // d, 2)
        d *= 2
    return out


def conv_chunk(xb, rows, u, mask_ref, bias_ref, xf, yf, put):
    images, ch, pixels = xb.shape
    pairs = pixels // LANES
    span = pairs + 3
    for i in range(images):
        x = xb[i].astype(jnp.float32)
        x = jnp.concatenate([x, jnp.zeros((ch, LANES), jnp.float32)], axis=1)
        x = pltpu.roll(x, W, axis=1)
        for g in range(pairs + 1):
            xf[pl.ds((i * span + g + 1) * ch, ch), :] = x[:, g * LANES : (g + 1) * LANES]
    mask = mask_ref[...]
    for c in range(ch):
        bands = []
        for s in range(KS + 1):
            first = jnp.broadcast_to(u[s, pl.ds(rows + c, 1), :], (W, LANES))
            band = pltpu.roll(first, 0, 1, stride=1, stride_axis=0) * mask
            bands.append(band.astype(jnp.bfloat16))
        parts = []
        for i in range(images):
            moved = [
                xf[pl.ds((i * span + j) * ch + c, pairs, stride=ch), :].astype(jnp.bfloat16)
                for j in range((KS + 1) // 2)
            ]
            parts.append(jnp.concatenate(moved, axis=1))
        y = jnp.dot(
            jnp.concatenate(parts, axis=0),
            jnp.concatenate(bands, axis=0),
            preferred_element_type=jnp.float32,
        )
        yf[pl.ds(c, images * pairs, stride=ch), :] = y + bias_ref[rows + c]
    for i in range(images):
        for g in range(pairs):
            put(i, g, yf[pl.ds((i * pairs + g) * ch, ch), :].astype(jnp.bfloat16))


def low_bit(x):
    return x & -x


def lower(x, n):
    hops = []
    d = (low_bit(x) if x else n) // 2
    while d >= 1:
        hops.append(d)
        d //= 2
    return hops


def fused_kernel(
    n,
    x_hbm,
    k_ref,
    bias_ref,
    table_ref,
    mask_ref,
    w_ref,
    scale_ref,
    cot_hbm,
    a_ref,
    b_ref,
    gain_ref,
    shift_ref,
    oa_ref,
    ob_ref,
    xb,
    u,
    xf,
    yf,
    stage,
    conv,
    weight,
    cot,
    tok,
    grads,
    ga_ref,
    gb_ref,
    pair,
    held,
    parts,
    total,
    x_sem,
    cot_sem,
    own_sem,
    early_send,
    early_recv,
    late_send,
    late_recv,
    w_send,
    w_recv,
    y_send,
    y_recv,
    f_send,
    f_recv,
    pair_sem,
    s1,
    r1,
    s2,
    r2,
):
    images, channels, pixels = x_hbm.shape
    piece = pixels // n
    hidden = w_ref.shape[1]
    depth = channels * n
    chunks = channels // CH
    quarter = channels // QUARTERS
    me = lax.axis_index("swap")
    core = lax.axis_index("image")
    other = 1 - core
    group = lax.axis_index("group")

    def x_load(q):
        slot = lax.rem(q, 2)
        return pltpu.make_async_copy(
            x_hbm.at[:, pl.ds(pl.multiple_of(q * CH, CH), CH), :], xb.at[slot], x_sem.at[slot]
        )

    def cot_load(unit):
        slot = lax.rem(unit, 2)
        image = lax.rem(core + lax.rem(unit, 2), 2) * images + unit // 2
        return pltpu.make_async_copy(cot_hbm.at[image], cot.at[slot], cot_sem.at[slot])

    x_load(0).start()
    x_load(1).start()
    barrier = pltpu.get_barrier_semaphore()
    for k in range(1, n):
        pl.semaphore_signal(
            barrier, inc=1, device_id={"swap": flip(me, k)}, device_id_type=MESH
        )
    pl.semaphore_signal(barrier, inc=1, device_id={"image": other}, device_id_type=MESH)
    pl.semaphore_signal(barrier, inc=1, device_id={"group": 1 - group}, device_id_type=MESH)

    groups = scale_ref.shape[0]
    size = hidden // groups
    my_rows = pl.ds(pl.multiple_of(me * channels, CH), channels)
    factor = power_table(scale_ref[...]).astype(jnp.bfloat16)
    for j in range(hidden // STEP):
        at = slice(j * STEP, (j + 1) * STEP)
        block = lax.broadcasted_iota(jnp.int32, (groups, STEP), 1) + j * STEP
        first = lax.broadcasted_iota(jnp.int32, (groups, STEP), 0) * size
        spread = jnp.where((block >= first) & (block < first + size), 1.0, 0.0)
        wide = lax.dot_general(
            factor,
            spread.astype(jnp.bfloat16),
            (((0,), (0,)), ((), ())),
            preferred_element_type=jnp.float32,
        )
        weight[my_rows, at] = (w_ref[:, at].astype(jnp.float32) * wide).astype(jnp.bfloat16)
    zero = jnp.zeros((CH, LANES), jnp.float32)
    span = pixels // LANES + 3
    for i in range(images):
        xf[pl.ds(i * span * CH, CH), :] = zero
        xf[pl.ds((i * span + span - 1) * CH, CH), :] = zero
    for s in range(KS + 1):
        u[s] = lax.dot_general(
            k_ref[...],
            table_ref[:, s * LANES : (s + 1) * LANES],
            (((0,), (0,)), ((), ())),
            preferred_element_type=jnp.float32,
        )
    ga_ref[...] = jnp.zeros_like(ga_ref)
    gb_ref[...] = jnp.zeros_like(gb_ref)
    weight[depth:, :] = b_ref[...]
    pl.semaphore_wait(barrier, n + 1)

    share = channels // 2

    def halved(x):
        return x >= n // 2 or (x % 2 == 1 and x != 1)

    bit = share // 2

    def pieces(x):
        return (0, 1) if halved(x) else (0, 1, 2)

    def w_piece(p):
        if p == 2:
            return (1 - group) * share, share
        return group * share + p * bit, bit

    def w_rows(x, p):
        start, count = w_piece(p)
        return pl.ds(pl.multiple_of(flip(me, x) * channels + start, CH), count)

    def w_move(x, d, p):
        rows = w_rows(x, p)
        return pltpu.make_async_remote_copy(
            src_ref=weight.at[rows],
            dst_ref=weight.at[rows],
            send_sem=w_send.at[x + d, p],
            recv_sem=w_recv.at[x + d, p],
            device_id={"swap": flip(me, d)},
            device_id_type=MESH,
        )

    def w_cross(x, p):
        rows = w_rows(x, p)
        return pltpu.make_async_remote_copy(
            src_ref=weight.at[rows],
            dst_ref=weight.at[rows],
            send_sem=y_send.at[x, p],
            recv_sem=y_recv.at[x, p],
            device_id={"group": 1 - group},
            device_id_type=MESH,
        )

    def w_crossed(x, p):
        start = flip(me, x) * channels + (1 - group) * share + p * bit
        rows = pl.ds(pl.multiple_of(start, CH), bit)
        return pltpu.make_async_remote_copy(
            src_ref=weight.at[rows],
            dst_ref=weight.at[rows],
            send_sem=y_send.at[x, p],
            recv_sem=y_recv.at[x, p],
            device_id={"group": 1 - group},
            device_id_type=MESH,
        )

    def w_came(x, p):
        rows = w_rows(x, p)
        return pltpu.make_async_remote_copy(
            src_ref=weight.at[rows],
            dst_ref=weight.at[rows],
            send_sem=w_send.at[x, p],
            recv_sem=w_recv.at[x, p],
            device_id={"swap": flip(me, low_bit(x))},
            device_id_type=MESH,
        )

    def passed(x, p):
        return [d for d in lower(x, n) if p in pieces(x + d)]

    def pass_on(x, p):
        w_came(x, p).wait_recv()
        for d in passed(x, p):
            w_move(x, d, p).start()
        if halved(x):
            w_cross(x, p).start()

    def early(q, i, k):
        peer = flip(me, k)
        return pltpu.make_async_remote_copy(
            src_ref=stage.at[i, peer, pl.ds(pl.multiple_of(q * quarter, CH), quarter)],
            dst_ref=conv.at[i, pl.ds(pl.multiple_of(me * channels + q * quarter, CH), quarter)],
            send_sem=early_send.at[q, i, k],
            recv_sem=early_recv.at[q, i, k],
            device_id={"swap": peer},
            device_id_type=MESH,
        )

    def late(i, k):
        peer = flip(me, k)
        return pltpu.make_async_remote_copy(
            src_ref=stage.at[i, peer],
            dst_ref=conv.at[i, my_rows],
            send_sem=late_send.at[i, k],
            recv_sem=late_recv.at[i, k],
            device_id={"swap": peer},
            device_id_type=MESH,
        )

    def own(i):
        return pltpu.make_async_copy(stage.at[i, me], conv.at[i, my_rows], own_sem.at[i])

    def forward(i):
        return pltpu.make_async_remote_copy(
            src_ref=tok.at[lax.rem(i, 2)],
            dst_ref=tok.at[2 + i],
            send_sem=f_send.at[i],
            recv_sem=f_recv.at[i],
            device_id={"image": other},
            device_id_type=MESH,
        )

    early_hops = [4,6]
    late_hops = [5,7,2,1,3]
    for d in lower(0, n):
        for p in pieces(d):
            w_move(0, d, p).start()
    cot_load(0).start()
    cot_load(1).start()
    order = sorted(range(2, n), key=lambda x: (bin(x).count("1"), -x))
    order = [(x, p) for x in order for p in pieces(x) if halved(x) or passed(x, p)]
    during = (2, 4, 7, 8, 10, 11)

    def chunk(q, carry):
        x_load(q).wait()
        rows = pl.multiple_of(q * CH, CH)
        per = piece // LANES

        def put(i, g, values):
            at = (g % per) * LANES
            stage[i, g // per, pl.ds(rows, CH), at : at + LANES] = values

        conv_chunk(xb.at[lax.rem(q, 2)], rows, u, mask_ref, bias_ref, xf, yf, put)

        @pl.when(q + 2 < chunks)
        def _():
            x_load(q + 2).start()

        for at, (x, p) in zip(during, order):

            @pl.when(q == at)
            def _():
                pass_on(x, p)

        per_quarter = chunks // QUARTERS

        @pl.when(lax.rem(q, per_quarter) == per_quarter - 1)
        def _():
            for i in range(3):
                for k in early_hops:
                    early(q // per_quarter, i, k).start()

        return carry

    lax.fori_loop(0, chunks, chunk, 0)
    for i in range(images):
        own(i).start()
    for x, p in order[len(during) :]:
        pass_on(x, p)
    for i in range(images):
        for k in late_hops:
            late(i, k).start()
        if i >= 3:
            for q in range(QUARTERS):
                for k in early_hops:
                    early(q, i, k).start()
    for x in range(1, n):
        if halved(x):
            for p in pieces(x):
                w_crossed(x, p).wait_recv()
        else:
            for p in pieces(x):
                if not passed(x, p):
                    w_came(x, p).wait_recv()

    rank = b_ref.shape[0]

    def normalise(i):
        for s in range(piece // LANES):
            at = slice(s * LANES, (s + 1) * LANES)
            x = conv[i, :, at].astype(jnp.float32)
            average = jnp.sum(x, axis=0, keepdims=True) * (1.0 / depth)
            centred = x - average
            variance = jnp.sum(centred * centred, axis=0, keepdims=True) * (1.0 / depth)
            scaled = jnp.swapaxes(centred * lax.rsqrt(variance + norm_eps), 0, 1)
            scaled = scaled * gain_ref[...][None, :] + shift_ref[...][None, :]
            tok[lax.rem(i, 2), at, :] = scaled.astype(jnp.bfloat16)

    def unit(v, carry):
        i = v // 2
        second = lax.rem(v, 2)

        @pl.when(second == 0)
        def _():
            @pl.when(i >= 2)
            def _():
                forward(i - 2).wait_send()

            own(i).wait()
            for k in early_hops:
                for q in range(QUARTERS):
                    early(q, i, k).wait_recv()
            for k in late_hops:
                late(i, k).wait_recv()
            normalise(i)
            forward(i).start()

        @pl.when(second == 1)
        def _():
            forward(i).wait_recv()

        cot_load(v).wait()
        slot = second * (2 + i) + (1 - second) * lax.rem(i, 2)
        tokens = tok[slot]
        low = lax.dot_general(
            tokens, a_ref[...], (((1,), (1,)), ((), ())), preferred_element_type=jnp.float32
        ).astype(jnp.bfloat16)
        wide = low.astype(jnp.float32)
        low_t = jnp.swapaxes(wide, 0, 1).astype(jnp.bfloat16)
        joined = jnp.concatenate([tokens, (adapter_scale * wide).astype(jnp.bfloat16)], axis=1)
        for j in range(hidden // STEP):
            at = slice(j * STEP, (j + 1) * STEP)
            pre = jnp.dot(joined, weight[:, at], preferred_element_type=jnp.float32)
            grad = cot[second, :, at].astype(jnp.float32) * gelu_slope(pre)
            grads[:, at] = grad.astype(jnp.bfloat16)
        grad = grads[...]
        back = lax.dot_general(
            b_ref[...], grad, (((1,), (1,)), ((), ())), preferred_element_type=jnp.float32
        )
        gb_ref[...] += adapter_scale * jnp.dot(low_t, grad, preferred_element_type=jnp.float32)
        high = back.astype(jnp.bfloat16)
        rest = back - high.astype(jnp.float32)
        middle = rest.astype(jnp.bfloat16)
        least = (rest - middle.astype(jnp.float32)).astype(jnp.bfloat16)
        three = jnp.dot(
            jnp.concatenate([high, middle, least], axis=0),
            tokens,
            preferred_element_type=jnp.float32,
        )
        ga_ref[...] += adapter_scale * (
            three[:rank] + three[rank : 2 * rank] + three[2 * rank :]
        )

        @pl.when(v + 2 < 2 * images)
        def _():
            cot_load(v + 2).start()

        return carry

    lax.fori_loop(0, 2 * images, unit, 0)
    sum_grads(n, ga_ref, gb_ref, oa_ref, ob_ref, pair, held, parts, total, pair_sem, s1, r1, s2, r2)
    for i in range(images):
        for k in early_hops:
            for q in range(QUARTERS):
                early(q, i, k).wait_send()
        for k in late_hops:
            late(i, k).wait_send()
    for i in range(max(images - 2, 0), images):
        forward(i).wait_send()
    for x in range(n):
        for d in lower(x, n):
            for p in pieces(x + d):
                w_move(x, d, p).wait_send()
        if halved(x):
            for p in pieces(x):
                w_cross(x, p).wait_send()


def sum_grads(n, ga_ref, gb_ref, oa_ref, ob_ref, pair, held, parts, total, pair_sem, s1, r1, s2, r2):
    me = lax.axis_index("swap")
    other = 1 - lax.axis_index("image")
    rank, wide_a = ga_ref.shape
    wide_b = gb_ref.shape[1]
    per = n // (rank // 8)
    ca, cb = wide_a // per, wide_b // per
    swap_a = pltpu.make_async_remote_copy(
        src_ref=ga_ref,
        dst_ref=pair,
        send_sem=pair_sem.at[0],
        recv_sem=pair_sem.at[1],
        device_id={"image": other},
        device_id_type=MESH,
    )
    swap_a.start()

    def place(ref, j, width):
        return ref.at[
            pl.ds(pl.multiple_of((j // per) * 8, 8), 8),
            pl.ds(pl.multiple_of((j % per) * width, 128), width),
        ]

    def move(src, dst, peer, ss, rs):
        return pltpu.make_async_remote_copy(
            src_ref=src,
            dst_ref=dst,
            send_sem=ss,
            recv_sem=rs,
            device_id={"swap": peer},
            device_id_type=MESH,
        )

    def scatter_b(k):
        peer = lax.rem(me + k, n)
        return move(
            place(gb_ref, peer, cb), parts.at[k, :, ca : ca + cb], peer, s1.at[1, k], r1.at[1, k]
        )

    def scatter_a(k):
        peer = lax.rem(me + k, n)
        return move(
            place(held, peer, ca), parts.at[k, :, 0:ca], peer, s1.at[0, k], r1.at[0, k]
        )

    for k in range(1, n):
        scatter_b(k).start()
    swap_a.wait()
    held[...] = ga_ref[...] + pair[...]
    for k in range(1, n):
        scatter_a(k).start()
    sum_b = place(gb_ref, me, cb)[...]
    for k in range(1, n):
        scatter_b(k).wait_recv()
        sum_b = sum_b + parts[k, :, ca : ca + cb]
    sum_a = place(held, me, ca)[...]
    for k in range(1, n):
        scatter_a(k).wait_recv()
        sum_a = sum_a + parts[k, :, 0:ca]
    total[:, 0:ca] = sum_a
    total[:, ca : ca + cb] = sum_b
    place(oa_ref, me, ca)[...] = sum_a
    place(ob_ref, me, cb)[...] = sum_b

    def gather_a(k):
        peer = lax.rem(me + k, n)
        return move(total.at[:, 0:ca], place(oa_ref, me, ca), peer, s2.at[0, k], r2.at[0, k])

    def gather_b(k):
        peer = lax.rem(me + k, n)
        return move(
            total.at[:, ca : ca + cb], place(ob_ref, me, cb), peer, s2.at[1, k], r2.at[1, k]
        )

    for k in range(1, n):
        gather_b(k).start()
        gather_a(k).start()
    for k in range(1, n):
        gather_b(k).wait_recv()
        gather_a(k).wait_recv()
    for k in range(1, n):
        scatter_a(k).wait_send()
        scatter_b(k).wait_send()
        gather_a(k).wait_send()
        gather_b(k).wait_send()


def fused(
    n, images_in, kernel, conv_bias, weight, scales, cotangent, adapter_a, adapter_b, gain, shift
):
    images, channels, pixels = images_in.shape
    piece = pixels // n
    hidden = weight.shape[1]
    rank = adapter_b.shape[0]
    depth = channels * n
    pairs = pixels // LANES
    per = n // (rank // 8)
    wide = depth // per + hidden // per
    dma = pltpu.SemaphoreType.DMA
    vmem = pl.BlockSpec(memory_space=pltpu.VMEM)
    hbm = pl.BlockSpec(memory_space=pltpu.HBM)
    smem = pl.BlockSpec(memory_space=pltpu.SMEM)
    bf16, f32 = jnp.bfloat16, jnp.float32
    return pl.pallas_call(
        functools.partial(fused_kernel, n),
        out_shape=(
            jax.ShapeDtypeStruct((rank, depth), f32),
            jax.ShapeDtypeStruct((rank, hidden), f32),
        ),
        in_specs=[hbm, vmem, smem, vmem, vmem, vmem, vmem, hbm, vmem, vmem, vmem, vmem],
        out_specs=(vmem, vmem),
        scratch_shapes=[
            pltpu.VMEM((2, images, CH, pixels), bf16),
            pltpu.VMEM((KS + 1, channels, LANES), f32),
            pltpu.VMEM((images * (pairs + 3) * CH, LANES), f32),
            pltpu.VMEM((images * pairs * CH, LANES), f32),
            pltpu.VMEM((images, n, channels, piece), bf16),
            pltpu.VMEM((images, depth, piece), bf16),
            pltpu.VMEM((depth + rank, hidden), bf16),
            pltpu.VMEM((2, piece, hidden), bf16),
            pltpu.VMEM((2 + images, piece, depth), bf16),
            pltpu.VMEM((piece, hidden), bf16),
            pltpu.VMEM((rank, depth), f32),
            pltpu.VMEM((rank, hidden), f32),
            pltpu.VMEM((rank, depth), f32),
            pltpu.VMEM((rank, depth), f32),
            pltpu.VMEM((n, 8, wide), f32),
            pltpu.VMEM((8, wide), f32),
            dma((2,)),
            dma((2,)),
            dma((images,)),
            dma((QUARTERS, images, n)),
            dma((QUARTERS, images, n)),
            dma((images, n)),
            dma((images, n)),
            dma((n, 3)),
            dma((n, 3)),
            dma((n, 2)),
            dma((n, 2)),
            dma((images,)),
            dma((images,)),
            dma((2,)),
            dma((2, n)),
            dma((2, n)),
            dma((2, n)),
            dma((2, n)),
        ],
        compiler_params=pltpu.CompilerParams(
            collective_id=0, has_side_effects=True, vmem_limit_bytes=62 * 2**20
        ),
        name="fused",
    )(
        images_in,
        kernel.T,
        conv_bias,
        jnp.asarray(band_table(), bf16),
        jnp.asarray(band_mask()),
        weight,
        scales.T,
        cotangent,
        adapter_a.T,
        adapter_b,
        gain,
        shift,
    )


def fast_shards(
    n,
    images_in,
    kernel,
    conv_bias,
    norm_gain,
    norm_shift,
    fp8_weight,
    block_scale,
    adapter_a,
    adapter_b,
    cotangent,
):
    grad_a, grad_b = fused(
        n,
        images_in,
        kernel,
        conv_bias,
        fp8_weight,
        block_scale,
        cotangent,
        adapter_a,
        adapter_b,
        norm_gain,
        norm_shift,
    )
    return (grad_a.T, grad_b)


def fits(n, images_in, fp8_weight, adapter_a):
    images, channels, pixels = images_in.shape
    rank = adapter_a.shape[1]
    piece = pixels // n
    per = n // (rank // 8) if rank % 8 == 0 else 0
    wide = fp8_weight.shape[1]
    return (
        per > 0
        and n >= 4
        and n & (n - 1) == 0
        and n % (rank // 8) == 0
        and rank % 16 == 0
        and channels % (2 * CH) == 0
        and channels % (QUARTERS * CH) == 0
        and pixels % n == 0
        and piece % LANES == 0
        and wide % STEP == 0
        and (channels * n) % (per * 128) == 0
        and wide % (per * 128) == 0
    )


def depthwise(images, kernel, conv_bias, map_width):
    batch, channels, pixels = images.shape
    maps = images.reshape(batch, channels, pixels // map_width, map_width)
    taps = kernel.reshape(channels, 1, KS, KS)
    half_span = KS // 2
    summed = lax.conv_general_dilated(
        maps,
        taps,
        (1, 1),
        ((half_span, half_span), (half_span, half_span)),
        dimension_numbers=("NCHW", "OIHW", "NCHW"),
        feature_group_count=channels,
        preferred_element_type=jnp.float32,
    )
    summed = summed.reshape(batch, channels, pixels)
    return summed + conv_bias[None, :, None]


def plain_shards(
    images_in,
    kernel,
    conv_bias,
    norm_gain,
    norm_shift,
    fp8_weight,
    block_scale,
    adapter_a,
    adapter_b,
    cotangent,
):
    conv = depthwise(images_in, kernel, conv_bias, W).astype(jnp.bfloat16)
    values = lax.all_to_all(conv, "swap", split_axis=2, concat_axis=1, tiled=True).astype(
        jnp.float32
    )
    average = jnp.mean(values, axis=1, keepdims=True)
    centred = values - average
    variance = jnp.mean(centred * centred, axis=1, keepdims=True)
    scaled = (
        centred * lax.rsqrt(variance + norm_eps) * norm_gain[None, :, None]
        + norm_shift[None, :, None]
    )
    normed = jnp.swapaxes(scaled, 1, 2).astype(jnp.bfloat16)
    own_rows = normed.reshape(-1, normed.shape[2])
    tokens = lax.all_gather(own_rows, "image", axis=0, tiled=True)
    zero_start = jnp.zeros((tokens.shape[0], fp8_weight.shape[1]), jnp.float32)
    local_weight = decode(fp8_weight, block_scale)
    shard_rows = lax.all_gather(local_weight, "swap", axis=0, tiled=True)
    columns = lax.slice_in_dim(tokens, 0, shard_rows.shape[0], axis=1)
    frozen = zero_start + jnp.dot(columns, shard_rows, preferred_element_type=jnp.float32)
    low_rank = jnp.dot(tokens, adapter_a, preferred_element_type=jnp.float32).astype(jnp.bfloat16)
    pre_act = frozen + adapter_scale * jnp.dot(
        low_rank, adapter_b, preferred_element_type=jnp.float32
    )
    upstream = cotangent.reshape(-1, cotangent.shape[2])
    grad_pre = (upstream.astype(jnp.float32) * gelu_slope(pre_act)).astype(jnp.bfloat16)
    grad_b_local = adapter_scale * jnp.dot(low_rank.T, grad_pre, preferred_element_type=jnp.float32)
    partial_back = jnp.dot(grad_pre, adapter_b.T, preferred_element_type=jnp.float32)
    contract = (((0,), (0,)), ((), ()))
    tokens_wide = tokens.astype(jnp.float32)
    summed_back = lax.psum(partial_back, "image")
    grad_a_local = adapter_scale * lax.dot_general(
        tokens_wide,
        summed_back,
        contract,
        precision=lax.Precision.HIGHEST,
        preferred_element_type=jnp.float32,
    )
    grad_a, grad_b = lax.psum((grad_a_local, grad_b_local), "swap")
    return (grad_a, grad_b)


def solution(mesh):
    placed = (
        P(("group", "image"), "swap", None),
        P("swap", None),
        P("swap"),
        P(),
        P(),
        P("swap", "image"),
        P("swap", "image"),
        P(),
        P(None, "image"),
        P("group", "swap", "image"),
    )
    n = mesh.shape["swap"]

    def shards(*arrays):
        if mesh.shape["image"] == 2 and mesh.shape["group"] == 2 and fits(n, arrays[0], arrays[5], arrays[7]):
            return fast_shards(n, *arrays)
        return plain_shards(*arrays)

    return jax.shard_map(
        shards,
        mesh=mesh,
        in_specs=placed,
        out_specs=(P("group", None), P("group", "image")),
        check_vma=False,
    )
```
